32 devices in a mesh: node: 8 (over z, x), mp: 4 (over y, core).
Axes of the slice: x: 2, y: 2, z: 4, core: 2. Of those that a mesh axis runs over, the one named last changes fastest.
Arguments:
- stored_features: float32 [16384, 1024], P('node', 'mp'), may hold values from -6 to 6
- vertex_row_index: int32 [16384], P('node'), may hold values from 0 to 511
- neighbors: int32 [2, 16384, 16], P(None, 'node'), may hold values from 0 to 511
- counts: int32 [2, 16384], P(None, 'node'), may hold values from 1 to 16
- self_w1: float32 [1024, 256], P('mp'), may hold values from -0.1875 to 0.1875
- neigh_w1: float32 [1024, 256], P('mp'), may hold values from -0.1875 to 0.1875
- self_w2: float32 [256, 256], replicated, may hold values from -0.375 to 0.375
- neigh_w2: float32 [256, 256], replicated, may hold values from -0.375 to 0.375
- upstream: float32 [32, 512, 256], P('node', 'mp'), may hold values from -6 to 6
Outputs:
- layer_out: float32 [32, 512, 256], P('node', 'mp')
- grad_self1: float32 [1024, 256], P('mp')
- grad_neigh1: float32 [1024, 256], P('mp')
- grad_self2: float32 [256, 256], replicated
- grad_neigh2: float32 [256, 256], replicated
The draws below stay inside these ranges and needn't reach their ends.
Inputs may be any that keep to these rules, and one draw needn't show every extreme that they name: Only the first counts[l, r] slots of neighbors[l, r] are used; neighbour and stored-row numbers refer to the node's own subgraph.
All inputs are finite; a program needn't handle non-finite values.
Results may differ from the reference program's by a relative error of at most 0.003.
Values sent between devices are 32-bit elements; how exact they have to be, the bound alone decides.
A program may use at most 64 MiB of HBM per device.

```python
import math
import jax
import jax.numpy as jnp
import numpy as np
from jax import lax

F = 1024
H = 256
K = 16
NB = 512
GRAPHS = 32
NODES = 16384


def place_ends(array, rng, smallest, high):
    longest = array.shape.index(max(array.shape))
    spots = []
    for shift in (0, 1):
        where = [jax.random.randint(jax.random.fold_in(rng, axis), (), 0, length) for axis, length in enumerate(array.shape)]
        where[longest] = (where[longest] + shift) % array.shape[longest]
        spots.append(tuple(where))
    return array.at[spots[0]].set(smallest).at[spots[1]].set(high)


def steps_of(own_key, shape, shards, least, top_value):
    def one(dim, parts):
        draws = jax.random.uniform(jax.random.fold_in(jax.random.fold_in(own_key, 6), dim), (parts,), jnp.float32, least / len(shards), top_value / len(shards))
        return jnp.repeat(jnp.exp(draws), shape[dim] // parts).reshape((-1,) + (1,) * (len(shape) - dim - 1))

    gain = one(*shards[0])
    for cut in shards[1:]:
        gain = gain * one(*cut)
    return gain


def cumulative_ranks(number_of, slope):
    loads = [(1 << 20) // math.isqrt(grade ** slope) + 1 for grade in range(1, number_of + 1)]
    width = 1 + sum(loads) // (1 << 30)
    return np.cumsum(np.array([max(1, weight // width) for weight in loads]))


def ranked_ids(rng, extent, count, lean):
    listing = cumulative_ranks(count, lean)
    ticket = jax.random.randint(jax.random.fold_in(rng, 1), extent, 0, int(listing[count - 1]))
    standing = jnp.searchsorted(jnp.asarray(listing, jnp.int32), ticket, side="right")
    return jax.random.permutation(jax.random.fold_in(rng, 2), count)[standing].astype(jnp.int32)


def gaussian(key, dims, width, limit, shards=(), kind=jnp.bfloat16):
    loudness = steps_of(key, dims, shards, -0.22, 0.18) if shards else 1.0
    drawn = jax.random.normal(key, dims, jnp.float32) * width * loudness
    return jnp.minimum(jnp.maximum(drawn, -limit), limit).astype(kind)


def setup_inputs(seed: int = 0) -> dict:
    keys = jax.random.split(jax.random.key(seed), 10)
    return {
        "stored_features": gaussian(keys[0], (NODES, F), 1.0, 6.0, ((0, 8), (1, 4)), jnp.float32),
        "vertex_row_index": place_ends(jax.random.randint(keys[1], (NODES,), 0, NB), jax.random.fold_in(keys[1], 1), 0, NB - 1).astype(jnp.int32),
        "neighbors": place_ends(ranked_ids(keys[2], (2, NODES, K), NB, 2), jax.random.fold_in(keys[2], 3), 0, NB - 1).astype(jnp.int32),
        "counts": place_ends(jax.random.randint(keys[3], (2, NODES), 1, K + 1), jax.random.fold_in(keys[3], 1), 1, K).astype(jnp.int32),
        "self_w1": gaussian(keys[4], (F, H), F ** -0.5, 0.1875, ((0, 4),), jnp.float32),
        "neigh_w1": gaussian(keys[5], (F, H), F ** -0.5, 0.1875, ((0, 4),), jnp.float32),
        "self_w2": gaussian(keys[6], (H, H), H ** -0.5, 0.375, (), jnp.float32),
        "neigh_w2": gaussian(keys[7], (H, H), H ** -0.5, 0.375, (), jnp.float32),
        "upstream": gaussian(keys[8], (GRAPHS, NB, H), 1.0, 6.0, ((0, 8), (1, 4)), jnp.float32),
    }


epsilon = 1e-05
precise = lax.Precision.HIGHEST

def neighbor_mean(source_rows, neighbor_ids, row_counts):
    picked = jnp.take(source_rows, neighbor_ids, axis=0)
    slot_ids = jnp.arange(neighbor_ids.shape[1], dtype=jnp.int32)
    row_mask = (slot_ids[None, :] < row_counts[:, None]).astype(jnp.float32)
    summed = lax.optimization_barrier(jnp.sum(picked * row_mask[:, :, None], axis=1))
    return summed / row_counts[:, None].astype(jnp.float32)

def normed(pre_act):
    activated = jax.nn.relu(pre_act)
    return activated * lax.rsqrt(lax.optimization_barrier(jnp.mean(activated * activated, axis=1, keepdims=True)) + epsilon)

def block_forward(weights, store_rows, node_rows, neighbor_ids, row_counts):
    self_one, neigh_one, self_two, neigh_two = weights
    features = jnp.take(store_rows, node_rows, axis=0)
    agg_zero = neighbor_mean(features, neighbor_ids[0], row_counts[0])
    hidden = normed(jnp.dot(features, self_one, precision=precise) + jnp.dot(agg_zero, neigh_one, precision=precise))
    agg_one = neighbor_mean(hidden, neighbor_ids[1], row_counts[1])
    return jnp.dot(hidden, self_two, precision=precise) + jnp.dot(agg_one, neigh_two, precision=precise)

def reference(stored_features, vertex_row_index, neighbors, counts, self_w1, neigh_w1, self_w2, neigh_w2, upstream):
    gradient_scale = 1.0 / math.sqrt(NODES)
    stores = stored_features.reshape(GRAPHS, NB, F)
    vertex_blocks = vertex_row_index.reshape(GRAPHS, NB)
    neighbor_blocks = jnp.transpose(neighbors.reshape(2, GRAPHS, NB, K), (1, 0, 2, 3))
    block_count = jnp.transpose(counts.reshape(2, GRAPHS, NB), (1, 0, 2))
    cotangents = upstream * gradient_scale
    weights = (self_w1, neigh_w1, self_w2, neigh_w2)

    def per_block(packed):
        store_rows, node_rows, neighbor_ids, row_counts, cotangent = packed

        def forward(params):
            return block_forward(params, store_rows, node_rows, neighbor_ids, row_counts)
        block_out, pullback = jax.vjp(forward, weights)
        grad_sets, = pullback(cotangent)
        return (block_out, grad_sets)
    outputs, grad_sets = lax.map(per_block, (stores, vertex_blocks, neighbor_blocks, block_count, cotangents))
    return (outputs, lax.optimization_barrier(jnp.sum(grad_sets[0], axis=0)), lax.optimization_barrier(jnp.sum(grad_sets[1], axis=0)), lax.optimization_barrier(jnp.sum(grad_sets[2], axis=0)), lax.optimization_barrier(jnp.sum(grad_sets[3], axis=0)))
```

```python
import functools
import math

import jax
import jax.numpy as jnp
from jax import lax
from jax.experimental import pallas as pl
from jax.experimental.pallas import tpu as pltpu
from jax.sharding import PartitionSpec as P

epsilon = 1e-05
precise = lax.Precision.HIGHEST


def adjacency(neighbor_ids, row_counts, width):
    row_total = neighbor_ids.shape[0]
    slot_positions = neighbor_ids.shape[1]
    tile_rows = min(128, row_total)
    tiles = row_total // tile_rows
    column_ids = jnp.arange(width, dtype=jnp.int32)
    slot_ids = jnp.arange(slot_positions, dtype=jnp.int32)
    slot_weight = (slot_ids[None, :] < row_counts[:, None]).astype(jnp.float32) / row_counts[
        :, None
    ].astype(jnp.float32)

    def one_tile(packed):
        tile_ids, tile_weight = packed
        hits = (tile_ids[:, :, None] == column_ids[None, None, :]).astype(jnp.float32)
        return jnp.sum(hits * tile_weight[:, :, None], axis=1)

    tiled = lax.map(
        one_tile,
        (
            neighbor_ids.reshape(tiles, tile_rows, slot_positions),
            slot_weight.reshape(tiles, tile_rows, slot_positions),
        ),
    )
    return tiled.reshape(row_total, width)


def normed_parts(pre_act):
    activated = jnp.maximum(pre_act, 0.0)
    inverse = lax.rsqrt(jnp.mean(activated * activated, axis=1, keepdims=True) + epsilon)
    return (activated * inverse, activated, inverse)


def norm_backward(hidden_grad, activated, inverse, pre_act):
    inner_sum = jnp.mean(hidden_grad * activated, axis=1, keepdims=True)
    act_grad = inverse * hidden_grad - activated * (inverse * inverse * inverse) * inner_sum
    return jnp.where(pre_act > 0, act_grad, 0.0)


def body(
    stored_features,
    vertex_row_index,
    neighbors,
    counts,
    self_w1,
    neigh_w1,
    self_w2,
    neigh_w2,
    upstream,
):
    mp_index = lax.axis_index("mp")
    sampled_graphs = upstream.shape[0]
    own_rows = upstream.shape[1]
    row_grand_total = vertex_row_index.shape[0] // sampled_graphs
    column_total = stored_features.shape[1]
    slot_positions = neighbors.shape[2]
    gradient_scale = 1.0 / math.sqrt(row_grand_total * sampled_graphs * lax.axis_size("node"))
    first_row = mp_index * own_rows
    stored_blocks = stored_features.reshape(sampled_graphs, row_grand_total, column_total)
    vertex_blocks = vertex_row_index.reshape(sampled_graphs, row_grand_total)
    neighbor_blocks = jnp.transpose(
        neighbors.reshape(2, sampled_graphs, row_grand_total, slot_positions), (1, 0, 2, 3)
    )
    block_count = jnp.transpose(counts.reshape(2, sampled_graphs, row_grand_total), (1, 0, 2))

    def one_graph(carry, packed):
        store_rows, node_rows, neighbor_ids, row_counts, cotangent = packed
        features = jnp.take(store_rows, node_rows, axis=0)
        adj_zero = adjacency(neighbor_ids[0], row_counts[0], row_grand_total)
        agg_zero = jnp.dot(adj_zero, features, precision=precise)
        own_ids = lax.dynamic_slice_in_dim(neighbor_ids[1], first_row, own_rows, 0)
        own_counts = lax.dynamic_slice_in_dim(row_counts[1], first_row, own_rows, 0)
        adj_own = adjacency(own_ids, own_counts, row_grand_total)
        scaled = cotangent * gradient_scale
        back_neigh = jnp.dot(scaled, neigh_w2.T, precision=precise)
        back_self = jnp.dot(scaled, self_w2.T, precision=precise)
        contrib = lax.dot_general(adj_own, back_neigh, (((0,), (0,)), ((), ())), precision=precise)
        rows_self = features
        rows_neigh = agg_zero
        pre_own = lax.psum_scatter(
            jnp.dot(rows_self, self_w1, precision=precise)
            + jnp.dot(rows_neigh, neigh_w1, precision=precise),
            "mp",
            scatter_dimension=0,
            tiled=True,
        )
        hidden_own, act_own, inverse_own = normed_parts(pre_own)
        hidden_all = lax.all_gather(hidden_own, "mp", axis=0, tiled=True)
        agg_one = jnp.dot(adj_own, hidden_all, precision=precise)
        hidden_grad = lax.psum_scatter(contrib, "mp", scatter_dimension=0, tiled=True) + back_self
        pre_grad = norm_backward(hidden_grad, act_own, inverse_own, pre_own)
        grad_piece = lax.all_gather(pre_grad, "mp", axis=0, tiled=True)
        rows_self = features
        rows_neigh = agg_zero
        step_self1 = carry[0] + jnp.dot(rows_self.T, grad_piece, precision=precise)
        step_neigh1 = carry[1] + jnp.dot(rows_neigh.T, grad_piece, precision=precise)
        graph_out = jnp.dot(hidden_own, self_w2, precision=precise) + jnp.dot(
            agg_one, neigh_w2, precision=precise
        )
        step_self2 = carry[2] + jnp.dot(hidden_own.T, scaled, precision=precise)
        step_neigh2 = carry[3] + jnp.dot(agg_one.T, scaled, precision=precise)
        return ((step_self1, step_neigh1, step_self2, step_neigh2), graph_out)

    zero_first = jnp.zeros(self_w1.shape, jnp.float32)
    zero_second = jnp.zeros(self_w2.shape, jnp.float32)
    totals, layer_out = lax.scan(
        one_graph,
        (zero_first, zero_first, zero_second, zero_second),
        (stored_blocks, vertex_blocks, neighbor_blocks, block_count, upstream),
    )
    grad_self1, grad_neigh1, grad_self2, grad_neigh2 = totals
    grad_self1, grad_neigh1, grad_self2, grad_neigh2 = lax.psum(
        (grad_self1, grad_neigh1, grad_self2, grad_neigh2), "node"
    )
    grad_self2, grad_neigh2 = lax.psum((grad_self2, grad_neigh2), "mp")
    return (layer_out, grad_self1, grad_neigh1, grad_self2, grad_neigh2)


f32 = jnp.float32
bf16 = jnp.bfloat16


def halves(value):
    high = value.astype(bf16)
    return high, (value - high.astype(f32)).astype(bf16)


def thirds(value):
    high = value.astype(bf16)
    rest = value - high.astype(f32)
    middle = rest.astype(bf16)
    return high, middle, (rest - middle.astype(f32)).astype(bf16)


def mul(left, right, dims=((1,), (0,))):
    return lax.dot_general(left, right, (dims, ((), ())), preferred_element_type=f32)


def mul3(left, right, dims=((1,), (0,))):
    return (
        mul(left[0], right[0], dims) + mul(left[1], right[0], dims) + mul(left[0], right[1], dims)
    )


def mul6(left, right):
    small = mul(left[2], right[0]) + mul(left[0], right[2]) + mul(left[1], right[1])
    return mul(left[0], right[0]) + (mul(left[0], right[1]) + mul(left[1], right[0]) + small)


def fused_kernel(
    node_total,
    slots,
    scale,
    store_ref,
    ids_ref,
    w1_ref,
    w2_ref,
    up_ref,
    out_ref,
    g1_ref,
    g2_ref,
    upg,
    part,
    pin,
    far,
    pg,
    xh,
    xl,
    xt,
    wh,
    wl,
    wt,
    onehot,
    adj,
    act_buf,
    g1acc,
    g2acc,
    g2in,
    q2,
    q2r,
    outg,
    g1x,
    g1h,
    g1z,
    q2x,
    q2h,
    q2z,
    send_sems,
    recv_sems,
):
    rows = upg.shape[0]
    own = up_ref.shape[1]
    cols = store_ref.shape[1]
    depth = node_total // 2
    node = lax.axis_index("node")
    member = lax.axis_index("mp")
    zc, xc = node // 2, node % 2
    yc, cc = member // 2, member % 2
    partner = yc * 2 + (1 - cc)
    across = (1 - yc) * 2 + cc
    diagonal = (1 - yc) * 2 + (1 - cc)
    peers = (partner, across, diagonal)
    x_peer = zc * 2 + (1 - xc)
    z_next = [((zc + d) % depth) for d in range(1, depth)]
    z_prev = [((zc + depth - d) % depth) for d in range(1, depth)]

    def target(node_id, member_id):
        return dict(device_id=(node_id, member_id), device_id_type=pl.DeviceIdType.MESH)

    counter = [0]

    def copy(source, dest, node_id, member_id):
        k = counter[0]
        counter[0] += 1
        return pltpu.make_async_remote_copy(
            src_ref=source,
            dst_ref=dest,
            send_sem=send_sems.at[k],
            recv_sem=recv_sems.at[k],
            **target(node_id, member_id),
        )

    barrier = pltpu.get_barrier_semaphore()
    for p in peers:
        pl.semaphore_signal(barrier, inc=1, **target(node, p))
    pl.semaphore_signal(barrier, inc=1, **target(x_peer, member))
    for z in z_next:
        pl.semaphore_signal(barrier, inc=1, **target(z * 2 + xc, member))
    pl.semaphore_wait(barrier, 4 + depth - 1)

    def block(index, size):
        return pl.ds(pl.multiple_of(index * size, size), size)

    up_copies = [copy(up_ref.at[p], upg.at[block(member, own)], node, p) for p in peers]
    for one in up_copies:
        one.start()
    upg[block(member, own)] = up_ref[member]
    wh[...], wl[...], wt[...] = thirds(w1_ref[...])

    tile = 64
    lanes = lax.broadcasted_iota(jnp.int32, (tile, rows), 1)

    def hits(picked, first):
        total = jnp.zeros((tile, rows), f32)
        for k in range(first, first + slots):
            total = total + jnp.where(picked[:, k : k + 1] == lanes, 1.0, 0.0)
        return total.astype(bf16)

    def build(graph, first, with_vertex):
        @pl.loop(0, rows // tile)
        def _(t):
            at = pl.ds(pl.multiple_of(graph * rows + t * tile, tile), tile)
            picked = ids_ref[at]
            to = block(t, tile)
            adj[to] = hits(picked, first)
            if with_vertex:
                v = 2 * slots
                onehot[to] = jnp.where(picked[:, v : v + 1] == lanes, 1.0, 0.0).astype(bf16)

    def reciprocal(graph, layer):
        k = 2 * slots + 1 + layer
        return 1.0 / ids_ref[block(graph, rows), k : k + 1].astype(f32)

    to_partner_a = copy(part.at[0], pin.at[0], node, partner)
    to_across = copy(part.at[1], far, node, across)
    to_partner_b = copy(part.at[2], pin.at[1], node, partner)

    @pl.loop(0, 4)
    def _(s):
        gy = yc + (1 - s // 2) * (1 - 2 * yc)
        gc = cc + (1 - s % 2) * (1 - 2 * cc)
        graph = gy * 2 + gc
        build(graph, 0, True)
        sh, sl, st = thirds(store_ref[block(graph, rows)])
        fh = mul(onehot[...], sh).astype(bf16)
        fl = mul(onehot[...], sl).astype(bf16)
        ft = mul(onehot[...], st).astype(bf16)
        xh[s, :, :cols] = fh
        xl[s, :, :cols] = fl
        xt[:, :cols] = ft
        agg = (mul(adj[...], ft) + mul(adj[...], fl) + mul(adj[...], fh)) * reciprocal(graph, 0)
        ah, al, at = thirds(agg)
        xt[:, cols:] = at
        xh[s, :, cols:] = ah
        xl[s, :, cols:] = al
        part[s] = mul6((xh[s], xl[s], xt[...]), (wh[...], wl[...], wt[...]))

        @pl.when(s == 0)
        def _():
            to_partner_a.start()

        @pl.when(s == 1)
        def _():
            to_partner_a.wait_recv()
            part[1] = part[1] + pin[0]
            to_across.start()

        @pl.when(s == 2)
        def _():
            to_partner_b.start()

    build(member, slots, False)
    shrink = reciprocal(member, 1)
    for one in up_copies:
        one.wait_recv()
    scaled = halves(upg[...] * scale)
    w2s = halves(w2_ref[: w2_ref.shape[0] // 2])
    w2n = halves(w2_ref[w2_ref.shape[0] // 2 :])
    nt = ((1,), (1,))
    tn = ((0,), (0,))
    back = halves(mul3(scaled, w2n, nt) * shrink)
    hidden_grad = mul3(scaled, w2s, nt) + mul(adj[...], back[0], tn) + mul(adj[...], back[1], tn)
    act_buf[...] = hidden_grad
    to_partner_b.wait_recv()
    near = part[3] + pin[1]
    to_across.wait_recv()
    pre = near + far[...]
    hidden, activated, inverse = normed_parts(pre)
    pg[3] = norm_backward(act_buf[...], activated, inverse, pre)
    pg_partner = copy(pg.at[3], pg.at[2], node, partner)
    pg_across = copy(pg.at[3], pg.at[1], node, across)
    pg_forward = copy(pg.at[1], pg.at[0], node, partner)
    pg_across.start()
    pg_partner.start()

    hid = halves(hidden)
    agg_one = halves((mul(adj[...], hid[0]) + mul(adj[...], hid[1])) * shrink)
    width = hidden.shape[1]
    scaled = halves(upg[...] * scale)
    g2acc[:width] = mul3(hid, scaled, tn)
    g2acc[width:] = mul3(agg_one, scaled, tn)
    quarter = g2acc.shape[0] // 4
    g2_copies = [
        copy(g2acc.at[block(p, quarter)], g2in.at[d], node, p) for d, p in enumerate(peers)
    ]
    for one in g2_copies:
        one.start()
    w2s = halves(w2_ref[:width])
    w2n = halves(w2_ref[width:])
    outg[...] = mul3(hid, w2s) + mul3(agg_one, w2n)
    out_copies = [copy(outg.at[block(p, own)], out_ref.at[member], node, p) for p in peers]
    for one in out_copies:
        one.start()
    out_ref[member] = outg[block(member, own)]

    g1acc[...] = jnp.zeros_like(g1acc)

    @pl.loop(0, 4)
    def _(t):
        s = 3 - t

        @pl.when(t == 1)
        def _():
            pg_partner.wait_recv()

        @pl.when(t == 2)
        def _():
            pg_across.wait_recv()
            pg_forward.start()

        @pl.when(t == 3)
        def _():
            pg_forward.wait_recv()

        g1acc[...] += mul3((xh[s], xl[s]), halves(pg[s]), tn)

    sets = []
    for full, x_in, half, z_in, result in (
        (q2, q2x, q2h, q2z, q2r),
        (g1acc, g1x, g1h, g1z, g1_ref),
    ):
        size = full.shape[0] // 2
        piece = size // depth
        x_copy = copy(full.at[block(1 - xc, size)], x_in, x_peer, member)
        z_copies = [
            copy(half.at[block(z, piece)], z_in.at[d], z * 2 + xc, member)
            for d, z in enumerate(z_next)
        ]
        mine = pl.ds(pl.multiple_of(xc * size + zc * piece, piece), piece)
        spread = [copy(result.at[mine], result.at[mine], z * 2 + xc, member) for z in z_next]
        echo = [copy(result.at[mine], result.at[mine], x_peer, member)]
        for z in z_prev:
            there = pl.ds(pl.multiple_of(xc * size + z * piece, piece), piece)
            echo.append(copy(result.at[there], result.at[there], x_peer, member))
        sets.append((full, x_in, half, z_in, result, size, piece, x_copy, z_copies, mine, spread, echo))

    def start_x(one):
        one[7].start()

    def start_z(one):
        full, x_in, half, z_in, result, size, piece, x_copy, z_copies = one[:9]
        x_copy.wait()
        half[...] = full[block(xc, size)] + x_in[...]
        for each in z_copies:
            each.start()

    def start_spread(one):
        full, x_in, half, z_in, result, size, piece, x_copy, z_copies, mine, spread, echo = one
        total = half[block(zc, piece)]
        for d, each in enumerate(z_copies):
            each.wait_recv()
            total = total + z_in[d]
        result[mine] = total
        for each in spread:
            each.start()
        echo[0].start()

    def relay(one):
        spread, echo = one[10:]
        for each, onward in zip(spread, echo[1:]):
            each.wait_recv()
            onward.start()

    def finish(one):
        z_copies, spread, echo = one[8], one[10], one[11]
        for each in echo:
            each.wait()
        for each in z_copies + spread:
            each.wait_send()

    start_x(sets[1])
    summed = g2acc[block(member, quarter)]
    for d, one in enumerate(g2_copies):
        one.wait_recv()
        summed = summed + g2in[d]
    q2[...] = summed
    start_x(sets[0])
    start_z(sets[1])
    start_z(sets[0])
    start_spread(sets[1])
    start_spread(sets[0])
    relay(sets[0])
    relay(sets[1])
    finish(sets[0])
    here = block(member, quarter)
    last = [copy(q2r, g2_ref.at[here], node, p) for p in peers]
    for one in last:
        one.start()
    g2_ref[here] = q2r[...]
    finish(sets[1])
    for one in up_copies + [to_partner_a, to_across, to_partner_b, pg_partner, pg_across, pg_forward]:
        one.wait_send()
    for one in g2_copies:
        one.wait_send()
    for one in out_copies + last:
        one.wait()


def fused(mesh_node):
    def run(stored, vertex, neighbors, counts, self_w1, neigh_w1, self_w2, neigh_w2, upstream):
        graphs, own, width = upstream.shape
        rows = vertex.shape[0] // graphs
        slots = neighbors.shape[2]
        cols = stored.shape[1]
        total = vertex.shape[0]
        used = lax.broadcasted_iota(jnp.int32, neighbors.shape, 2) < counts[:, :, None]
        masked = jnp.where(used, neighbors, -1)
        ids = jnp.concatenate(
            [masked[0], masked[1], vertex[:, None], counts[0][:, None], counts[1][:, None]], axis=1
        )
        w1 = jnp.concatenate([self_w1, neigh_w1], axis=0)
        w2 = jnp.concatenate([self_w2, neigh_w2], axis=0)
        scale = 1.0 / math.sqrt(total * mesh_node)
        depth = mesh_node // 2
        wide = 2 * cols
        quarter = 2 * width // 4
        copies = 18 + 2 * (2 + 3 * (depth - 1))
        vm = pltpu.VMEM
        scratch = [
            vm((rows, width), f32),
            vm((4, rows, width), f32),
            vm((2, rows, width), f32),
            vm((rows, width), f32),
            vm((4, rows, width), f32),
            vm((4, rows, wide), bf16),
            vm((4, rows, wide), bf16),
            vm((rows, wide), bf16),
            vm((wide, width), bf16),
            vm((wide, width), bf16),
            vm((wide, width), bf16),
            vm((rows, rows), bf16),
            vm((rows, rows), bf16),
            vm((rows, width), f32),
            vm((wide, width), f32),
            vm((2 * width, width), f32),
            vm((3, quarter, width), f32),
            vm((quarter, width), f32),
            vm((quarter, width), f32),
            vm((rows, width), f32),
            vm((wide // 2, width), f32),
            vm((wide // 2, width), f32),
            vm((depth - 1, wide // 2 // depth, width), f32),
            vm((quarter // 2, width), f32),
            vm((quarter // 2, width), f32),
            vm((depth - 1, quarter // 2 // depth, width), f32),
            pltpu.SemaphoreType.DMA((copies,)),
            pltpu.SemaphoreType.DMA((copies,)),
        ]
        space = pl.BlockSpec(memory_space=pltpu.VMEM)
        out, g1, g2 = pl.pallas_call(
            functools.partial(fused_kernel, mesh_node, slots, scale),
            out_shape=(
                jax.ShapeDtypeStruct((graphs, own, width), f32),
                jax.ShapeDtypeStruct((wide, width), f32),
                jax.ShapeDtypeStruct((2 * width, width), f32),
            ),
            in_specs=[space] * 5,
            out_specs=(space,) * 3,
            scratch_shapes=scratch,
            compiler_params=pltpu.CompilerParams(
                collective_id=0, has_side_effects=True, vmem_limit_bytes=60 * 1024 * 1024
            ),
        )(stored, ids, w1, w2, upstream)
        return out, g1[:cols], g1[cols:], g2[:width], g2[width:]

    return run


def fitted(mesh):
    node_total, members = mesh.shape["node"], mesh.shape["mp"]

    def run(*args):
        vertex, upstream, stored = args[1], args[8], args[0]
        graphs, own, width = upstream.shape
        depth = node_total // 2
        fits = (
            members == 4
            and graphs == members
            and node_total % 2 == 0
            and depth > 1
            and own * members * graphs == vertex.shape[0]
            and own % 64 == 0
            and width % 128 == 0
            and stored.shape[1] % 128 == 0
            and (width // 4) % (8 * depth) == 0
            and stored.shape[1] % (8 * depth) == 0
        )
        return (fused(node_total) if fits else body)(*args)

    return run


def solution(mesh):
    placed = (
        P("node", "mp"),
        P("node"),
        P(None, "node", None),
        P(None, "node"),
        P("mp", None),
        P("mp", None),
        P(),
        P(),
        P("node", "mp", None),
    )
    return jax.shard_map(
        fitted(mesh),
        mesh=mesh,
        in_specs=placed,
        out_specs=(P("node", "mp", None), P("mp", None), P("mp", None), P(), P()),
        check_vma=False,
    )
```

```python
import functools
import math

import jax
import jax.numpy as jnp
from jax import lax
from jax.experimental import pallas as pl
from jax.experimental.pallas import tpu as pltpu
from jax.sharding import PartitionSpec as P

epsilon = 1e-05
precise = lax.Precision.HIGHEST


def adjacency(neighbor_ids, row_counts, width):
    row_total = neighbor_ids.shape[0]
    slot_positions = neighbor_ids.shape[1]
    tile_rows = min(128, row_total)
    tiles = row_total // tile_rows
    column_ids = jnp.arange(width, dtype=jnp.int32)
    slot_ids = jnp.arange(slot_positions, dtype=jnp.int32)
    slot_weight = (slot_ids[None, :] < row_counts[:, None]).astype(jnp.float32) / row_counts[
        :, None
    ].astype(jnp.float32)

    def one_tile(packed):
        tile_ids, tile_weight = packed
        hits = (tile_ids[:, :, None] == column_ids[None, None, :]).astype(jnp.float32)
        return jnp.sum(hits * tile_weight[:, :, None], axis=1)

    tiled = lax.map(
        one_tile,
        (
            neighbor_ids.reshape(tiles, tile_rows, slot_positions),
            slot_weight.reshape(tiles, tile_rows, slot_positions),
        ),
    )
    return tiled.reshape(row_total, width)


def normed_parts(pre_act):
    activated = jnp.maximum(pre_act, 0.0)
    inverse = lax.rsqrt(jnp.mean(activated * activated, axis=1, keepdims=True) + epsilon)
    return (activated * inverse, activated, inverse)


def norm_backward(hidden_grad, activated, inverse, pre_act):
    inner_sum = jnp.mean(hidden_grad * activated, axis=1, keepdims=True)
    act_grad = inverse * hidden_grad - activated * (inverse * inverse * inverse) * inner_sum
    return jnp.where(pre_act > 0, act_grad, 0.0)


def body(
    stored_features,
    vertex_row_index,
    neighbors,
    counts,
    self_w1,
    neigh_w1,
    self_w2,
    neigh_w2,
    upstream,
):
    mp_index = lax.axis_index("mp")
    sampled_graphs = upstream.shape[0]
    own_rows = upstream.shape[1]
    row_grand_total = vertex_row_index.shape[0] // sampled_graphs
    column_total = stored_features.shape[1]
    slot_positions = neighbors.shape[2]
    gradient_scale = 1.0 / math.sqrt(row_grand_total * sampled_graphs * lax.axis_size("node"))
    first_row = mp_index * own_rows
    stored_blocks = stored_features.reshape(sampled_graphs, row_grand_total, column_total)
    vertex_blocks = vertex_row_index.reshape(sampled_graphs, row_grand_total)
    neighbor_blocks = jnp.transpose(
        neighbors.reshape(2, sampled_graphs, row_grand_total, slot_positions), (1, 0, 2, 3)
    )
    block_count = jnp.transpose(counts.reshape(2, sampled_graphs, row_grand_total), (1, 0, 2))

    def one_graph(carry, packed):
        store_rows, node_rows, neighbor_ids, row_counts, cotangent = packed
        features = jnp.take(store_rows, node_rows, axis=0)
        adj_zero = adjacency(neighbor_ids[0], row_counts[0], row_grand_total)
        agg_zero = jnp.dot(adj_zero, features, precision=precise)
        own_ids = lax.dynamic_slice_in_dim(neighbor_ids[1], first_row, own_rows, 0)
        own_counts = lax.dynamic_slice_in_dim(row_counts[1], first_row, own_rows, 0)
        adj_own = adjacency(own_ids, own_counts, row_grand_total)
        scaled = cotangent * gradient_scale
        back_neigh = jnp.dot(scaled, neigh_w2.T, precision=precise)
        back_self = jnp.dot(scaled, self_w2.T, precision=precise)
        contrib = lax.dot_general(adj_own, back_neigh, (((0,), (0,)), ((), ())), precision=precise)
        rows_self = features
        rows_neigh = agg_zero
        pre_own = lax.psum_scatter(
            jnp.dot(rows_self, self_w1, precision=precise)
            + jnp.dot(rows_neigh, neigh_w1, precision=precise),
            "mp",
            scatter_dimension=0,
            tiled=True,
        )
        hidden_own, act_own, inverse_own = normed_parts(pre_own)
        hidden_all = lax.all_gather(hidden_own, "mp", axis=0, tiled=True)
        agg_one = jnp.dot(adj_own, hidden_all, precision=precise)
        hidden_grad = lax.psum_scatter(contrib, "mp", scatter_dimension=0, tiled=True) + back_self
        pre_grad = norm_backward(hidden_grad, act_own, inverse_own, pre_own)
        grad_piece = lax.all_gather(pre_grad, "mp", axis=0, tiled=True)
        rows_self = features
        rows_neigh = agg_zero
        step_self1 = carry[0] + jnp.dot(rows_self.T, grad_piece, precision=precise)
        step_neigh1 = carry[1] + jnp.dot(rows_neigh.T, grad_piece, precision=precise)
        graph_out = jnp.dot(hidden_own, self_w2, precision=precise) + jnp.dot(
            agg_one, neigh_w2, precision=precise
        )
        step_self2 = carry[2] + jnp.dot(hidden_own.T, scaled, precision=precise)
        step_neigh2 = carry[3] + jnp.dot(agg_one.T, scaled, precision=precise)
        return ((step_self1, step_neigh1, step_self2, step_neigh2), graph_out)

    zero_first = jnp.zeros(self_w1.shape, jnp.float32)
    zero_second = jnp.zeros(self_w2.shape, jnp.float32)
    totals, layer_out = lax.scan(
        one_graph,
        (zero_first, zero_first, zero_second, zero_second),
        (stored_blocks, vertex_blocks, neighbor_blocks, block_count, upstream),
    )
    grad_self1, grad_neigh1, grad_self2, grad_neigh2 = totals
    grad_self1, grad_neigh1, grad_self2, grad_neigh2 = lax.psum(
        (grad_self1, grad_neigh1, grad_self2, grad_neigh2), "node"
    )
    grad_self2, grad_neigh2 = lax.psum((grad_self2, grad_neigh2), "mp")
    return (layer_out, grad_self1, grad_neigh1, grad_self2, grad_neigh2)


f32 = jnp.float32
bf16 = jnp.bfloat16


def halves(value):
    high = value.astype(bf16)
    return high, (value - high.astype(f32)).astype(bf16)


def thirds(value):
    high = value.astype(bf16)
    rest = value - high.astype(f32)
    middle = rest.astype(bf16)
    return high, middle, (rest - middle.astype(f32)).astype(bf16)


def mul(left, right, dims=((1,), (0,))):
    return lax.dot_general(left, right, (dims, ((), ())), preferred_element_type=f32)


def mul3(left, right, dims=((1,), (0,))):
    return (
        mul(left[0], right[0], dims) + mul(left[1], right[0], dims) + mul(left[0], right[1], dims)
    )


def mul6(left, right):
    small = mul(left[2], right[0]) + mul(left[0], right[2]) + mul(left[1], right[1])
    return mul(left[0], right[0]) + (mul(left[0], right[1]) + mul(left[1], right[0]) + small)


def fused_kernel(
    node_total,
    slots,
    scale,
    store_ref,
    ids_ref,
    s1_ref,
    n1_ref,
    s2_ref,
    n2_ref,
    up_ref,
    out_ref,
    g1_ref,
    g2_ref,
    upg,
    part,
    pin,
    far,
    pg,
    xh,
    xl,
    xt,
    wh,
    wl,
    wt,
    onehot,
    adj,
    act_buf,
    g1acc,
    g2acc,
    g2in,
    q2,
    q2r,
    outg,
    xin,
    xhalf,
    zin,
    send_sems,
    recv_sems,
):
    rows = upg.shape[0]
    own = up_ref.shape[1]
    cols = store_ref.shape[1]
    depth = node_total // 2
    node = lax.axis_index("node")
    member = lax.axis_index("mp")
    zc, xc = node // 2, node % 2
    yc, cc = member // 2, member % 2
    partner = yc * 2 + (1 - cc)
    across = (1 - yc) * 2 + cc
    diagonal = (1 - yc) * 2 + (1 - cc)
    peers = (partner, across, diagonal)
    x_peer = zc * 2 + (1 - xc)
    z_next = [((zc + d) % depth) for d in range(1, depth)]
    z_prev = [((zc + depth - d) % depth) for d in range(1, depth)]

    def target(node_id, member_id):
        return dict(device_id=(node_id, member_id), device_id_type=pl.DeviceIdType.MESH)

    counter = [0]

    def copy(source, dest, node_id, member_id):
        k = counter[0]
        counter[0] += 1
        return pltpu.make_async_remote_copy(
            src_ref=source,
            dst_ref=dest,
            send_sem=send_sems.at[k],
            recv_sem=recv_sems.at[k],
            **target(node_id, member_id),
        )

    barrier = pltpu.get_barrier_semaphore()
    for p in peers:
        pl.semaphore_signal(barrier, inc=1, **target(node, p))
    pl.semaphore_signal(barrier, inc=1, **target(x_peer, member))
    for z in z_next:
        pl.semaphore_signal(barrier, inc=1, **target(z * 2 + xc, member))
    pl.semaphore_wait(barrier, 4 + depth - 1)

    def block(index, size):
        return pl.ds(pl.multiple_of(index * size, size), size)

    up_copies = [copy(up_ref.at[p], upg.at[block(member, own)], node, p) for p in peers]
    for one in up_copies:
        one.start()
    upg[block(member, own)] = up_ref[member]
    wh[:cols], wl[:cols], wt[:cols] = thirds(s1_ref[...])
    wh[cols:], wl[cols:], wt[cols:] = thirds(n1_ref[...])

    tile = 64
    middle = rows // 2
    lanes = (lax.broadcasted_iota(jnp.int32, (tile, rows), 1) - middle).astype(f32).astype(bf16)
    one_b, none_b = jnp.ones((), bf16), jnp.zeros((), bf16)

    def hits(picked, first):
        total = jnp.zeros((tile, rows), bf16)
        for k in range(first, first + slots):
            total = total + jnp.where(picked[:, k : k + 1] == lanes, one_b, none_b)
        return total

    def build(graph, first, with_vertex):
        @pl.loop(0, rows // tile)
        def _(t):
            at = pl.ds(pl.multiple_of(graph * rows + t * tile, tile), tile)
            picked = (ids_ref[at] - middle).astype(f32).astype(bf16)
            to = block(t, tile)
            adj[to] = hits(picked, first)
            if with_vertex:
                v = 2 * slots
                onehot[to] = jnp.where(picked[:, v : v + 1] == lanes, one_b, none_b)

    def reciprocal(graph, layer):
        k = 2 * slots + 1 + layer
        return 1.0 / ids_ref[block(graph, rows), k : k + 1].astype(f32)

    to_partner_a = copy(part.at[0], pin.at[0], node, partner)
    to_across = copy(part.at[1], far, node, across)
    to_partner_b = copy(part.at[2], pin.at[1], node, partner)

    @pl.loop(0, 4)
    def _(s):
        gy = yc + (1 - s // 2) * (1 - 2 * yc)
        gc = cc + (1 - s % 2) * (1 - 2 * cc)
        graph = gy * 2 + gc
        build(graph, 0, True)
        sh, sl, st = thirds(store_ref[block(graph, rows)])
        fh = mul(onehot[...], sh).astype(bf16)
        fl = mul(onehot[...], sl).astype(bf16)
        ft = mul(onehot[...], st).astype(bf16)
        xh[s, :, :cols] = fh
        xl[s, :, :cols] = fl
        xt[:, :cols] = ft
        agg = (mul(adj[...], ft) + mul(adj[...], fl) + mul(adj[...], fh)) * reciprocal(graph, 0)
        ah, al, at = thirds(agg)
        xt[:, cols:] = at
        xh[s, :, cols:] = ah
        xl[s, :, cols:] = al
        part[s] = mul6((xh[s], xl[s], xt[...]), (wh[...], wl[...], wt[...]))

        @pl.when(s == 0)
        def _():
            to_partner_a.start()

        @pl.when(s == 1)
        def _():
            to_partner_a.wait_recv()
            part[1] = part[1] + pin[0]
            to_across.start()

        @pl.when(s == 2)
        def _():
            to_partner_b.start()

    build(member, slots, False)
    shrink = reciprocal(member, 1)
    for one in up_copies:
        one.wait_recv()
    scaled = halves(upg[...] * scale)
    w2s = halves(s2_ref[...])
    w2n = halves(n2_ref[...])
    nt = ((1,), (1,))
    tn = ((0,), (0,))
    back = halves(mul3(scaled, w2n, nt) * shrink)
    hidden_grad = mul3(scaled, w2s, nt) + mul(adj[...], back[0], tn) + mul(adj[...], back[1], tn)
    act_buf[...] = hidden_grad
    to_partner_b.wait_recv()
    near = part[3] + pin[1]
    to_across.wait_recv()
    pre = near + far[...]
    hidden, activated, inverse = normed_parts(pre)
    pg[3] = norm_backward(act_buf[...], activated, inverse, pre)
    pg_partner = copy(pg.at[3], pg.at[2], node, partner)
    parts = [pl.ds(i * own, own) for i in range(4)]
    pg_across = [copy(pg.at[3, r], pg.at[1, r], node, across) for r in parts]
    pg_forward = [copy(pg.at[1, r], pg.at[0, r], node, partner) for r in parts]
    for one in pg_across:
        one.start()
    pg_partner.start()

    hid = halves(hidden)
    agg_one = halves((mul(adj[...], hid[0]) + mul(adj[...], hid[1])) * shrink)
    width = hidden.shape[1]
    scaled = halves(upg[...] * scale)
    g2acc[:width] = mul3(hid, scaled, tn)
    g2acc[width:] = mul3(agg_one, scaled, tn)
    quarter = g2acc.shape[0] // 4
    g2_copies = [
        copy(g2acc.at[block(p, quarter)], g2in.at[d], node, p) for d, p in enumerate(peers)
    ]
    for one in g2_copies:
        one.start()
    w2s = halves(s2_ref[...])
    w2n = halves(n2_ref[...])
    outg[...] = mul3(hid, w2s) + mul3(agg_one, w2n)
    out_copies = [copy(outg.at[block(p, own)], out_ref.at[member], node, p) for p in peers]
    for one in out_copies:
        one.start()
    out_ref[member] = outg[block(member, own)]

    g1acc[...] = jnp.zeros_like(g1acc)

    @pl.loop(0, 4)
    def _(t):
        s = 3 - t

        @pl.when(t == 1)
        def _():
            pg_partner.wait_recv()

        @pl.when(t == 2)
        def _():
            for one, onward in zip(pg_across, pg_forward):
                one.wait_recv()
                onward.start()

        @pl.when(t == 3)
        def _():
            for one in pg_forward:
                one.wait_recv()

        g1acc[...] += mul3((xh[s], xl[s]), halves(pg[s]), tn)

    sets = []
    chunk = q2.shape[0]
    pieces = g1acc.shape[0] // chunk
    for full, base, i, result in [(g1acc, e * chunk, e, g1_ref) for e in range(pieces)] + [
        (q2, 0, pieces, q2r)
    ]:
        size = chunk // 2
        piece = size // depth
        x_in, half, z_in = xin.at[i], xhalf.at[i], zin.at[i]
        away = pl.ds(pl.multiple_of(base + (1 - xc) * size, size), size)
        home = pl.ds(pl.multiple_of(base + xc * size, size), size)
        x_copy = copy(full.at[away], x_in, x_peer, member)
        z_copies = [
            copy(xhalf.at[i, block(z, piece)], zin.at[i, d], z * 2 + xc, member)
            for d, z in enumerate(z_next)
        ]
        mine = pl.ds(pl.multiple_of(base + xc * size + zc * piece, piece), piece)
        spread = [copy(result.at[mine], result.at[mine], z * 2 + xc, member) for z in z_next]
        echo = [copy(result.at[mine], result.at[mine], x_peer, member)]
        for z in z_prev:
            there = pl.ds(pl.multiple_of(base + xc * size + z * piece, piece), piece)
            echo.append(copy(result.at[there], result.at[there], x_peer, member))
        sets.append((full, home, i, piece, result, x_copy, z_copies, mine, spread, echo))

    def start_z(one):
        full, home, i, piece, result, x_copy, z_copies = one[:7]
        x_copy.wait()
        xhalf[i] = full[home] + xin[i]
        for each in z_copies:
            each.start()

    def start_spread(one):
        full, home, i, piece, result, x_copy, z_copies, mine, spread, echo = one
        total = xhalf[i, block(zc, piece)]
        for d, each in enumerate(z_copies):
            each.wait_recv()
            total = total + zin[i, d]
        result[mine] = total
        for each in spread:
            each.start()
        echo[0].start()

    def relay(one):
        for each, onward in zip(one[8], one[9][1:]):
            each.wait_recv()
            onward.start()

    def finish(one):
        for each in one[9]:
            each.wait()
        for each in one[6] + one[8]:
            each.wait_send()

    first, second = sets[:-1], sets[-1]
    for one in first:
        one[5].start()
    for one in first[:-1]:
        start_z(one)
    summed = g2acc[block(member, quarter)]
    for d, one in enumerate(g2_copies):
        one.wait_recv()
        summed = summed + g2in[d]
    q2[...] = summed
    second[5].start()
    start_z(first[-1])
    for one in first:
        start_spread(one)
    start_z(second)
    for one in first:
        relay(one)
    start_spread(second)
    relay(second)
    finish(second)
    here = block(member, quarter)
    last = [copy(q2r, g2_ref.at[here], node, p) for p in peers]
    for one in last:
        one.start()
    g2_ref[here] = q2r[...]
    for one in first:
        finish(one)
    for one in up_copies + [to_partner_a, to_across, to_partner_b, pg_partner] + pg_across + pg_forward:
        one.wait_send()
    for one in g2_copies:
        one.wait_send()
    for one in out_copies + last:
        one.wait()


def fused(mesh_node):
    def run(stored, vertex, neighbors, counts, self_w1, neigh_w1, self_w2, neigh_w2, upstream):
        graphs, own, width = upstream.shape
        rows = vertex.shape[0] // graphs
        slots = neighbors.shape[2]
        cols = stored.shape[1]
        total = vertex.shape[0]
        used = lax.broadcasted_iota(jnp.int32, neighbors.shape, 2) < counts[:, :, None]
        masked = jnp.where(used, neighbors, 4 * rows)
        ids = jnp.concatenate(
            [masked[0], masked[1], vertex[:, None], counts[0][:, None], counts[1][:, None]], axis=1
        )
        scale = 1.0 / math.sqrt(total * mesh_node)
        depth = mesh_node // 2
        wide = 2 * cols
        quarter = 2 * width // 4
        groups = wide // quarter + 1
        copies = 24 + groups * (2 + 3 * (depth - 1))
        vm = pltpu.VMEM
        scratch = [
            vm((rows, width), f32),
            vm((4, rows, width), f32),
            vm((2, rows, width), f32),
            vm((rows, width), f32),
            vm((4, rows, width), f32),
            vm((4, rows, wide), bf16),
            vm((4, rows, wide), bf16),
            vm((rows, wide), bf16),
            vm((wide, width), bf16),
            vm((wide, width), bf16),
            vm((wide, width), bf16),
            vm((rows, rows), bf16),
            vm((rows, rows), bf16),
            vm((rows, width), f32),
            vm((wide, width), f32),
            vm((2 * width, width), f32),
            vm((3, quarter, width), f32),
            vm((quarter, width), f32),
            vm((quarter, width), f32),
            vm((rows, width), f32),
            vm((groups, quarter // 2, width), f32),
            vm((groups, quarter // 2, width), f32),
            vm((groups, depth - 1, quarter // 2 // depth, width), f32),
            pltpu.SemaphoreType.DMA((copies,)),
            pltpu.SemaphoreType.DMA((copies,)),
        ]
        space = pl.BlockSpec(memory_space=pltpu.VMEM)
        out, g1, g2 = pl.pallas_call(
            functools.partial(fused_kernel, mesh_node, slots, scale),
            out_shape=(
                jax.ShapeDtypeStruct((graphs, own, width), f32),
                jax.ShapeDtypeStruct((wide, width), f32),
                jax.ShapeDtypeStruct((2 * width, width), f32),
            ),
            in_specs=[space] * 7,
            out_specs=(space,) * 3,
            scratch_shapes=scratch,
            compiler_params=pltpu.CompilerParams(
                collective_id=0, has_side_effects=True, vmem_limit_bytes=60 * 1024 * 1024
            ),
        )(stored, ids, self_w1, neigh_w1, self_w2, neigh_w2, upstream)
        return out, g1[:cols], g1[cols:], g2[:width], g2[width:]

    return run


def fitted(mesh):
    node_total, members = mesh.shape["node"], mesh.shape["mp"]

    def run(*args):
        vertex, upstream, stored = args[1], args[8], args[0]
        graphs, own, width = upstream.shape
        depth = node_total // 2
        fits = (
            members == 4
            and graphs == members
            and node_total % 2 == 0
            and depth > 1
            and own * members * graphs == vertex.shape[0]
            and own % 64 == 0
            and own * members <= 512
            and width % 128 == 0
            and stored.shape[1] % 128 == 0
            and (width // 4) % (8 * depth) == 0
            and (2 * stored.shape[1]) % (width // 2) == 0
        )
        return (fused(node_total) if fits else body)(*args)

    return run


def solution(mesh):
    placed = (
        P("node", "mp"),
        P("node"),
        P(None, "node", None),
        P(None, "node"),
        P("mp", None),
        P("mp", None),
        P(),
        P(),
        P("node", "mp", None),
    )
    return jax.shard_map(
        fitted(mesh),
        mesh=mesh,
        in_specs=placed,
        out_specs=(P("node", "mp", None), P("mp", None), P("mp", None), P(), P()),
        check_vma=False,
    )
```

```python
import functools
import math

import jax
import jax.numpy as jnp
from jax import lax
from jax.experimental import pallas as pl
from jax.experimental.pallas import tpu as pltpu
from jax.sharding import PartitionSpec as P

epsilon = 1e-05
precise = lax.Precision.HIGHEST


def adjacency(neighbor_ids, row_counts, width):
    row_total = neighbor_ids.shape[0]
    slot_positions = neighbor_ids.shape[1]
    tile_rows = min(128, row_total)
    tiles = row_total // tile_rows
    column_ids = jnp.arange(width, dtype=jnp.int32)
    slot_ids = jnp.arange(slot_positions, dtype=jnp.int32)
    slot_weight = (slot_ids[None, :] < row_counts[:, None]).astype(jnp.float32) / row_counts[
        :, None
    ].astype(jnp.float32)

    def one_tile(packed):
        tile_ids, tile_weight = packed
        hits = (tile_ids[:, :, None] == column_ids[None, None, :]).astype(jnp.float32)
        return jnp.sum(hits * tile_weight[:, :, None], axis=1)

    tiled = lax.map(
        one_tile,
        (
            neighbor_ids.reshape(tiles, tile_rows, slot_positions),
            slot_weight.reshape(tiles, tile_rows, slot_positions),
        ),
    )
    return tiled.reshape(row_total, width)


def normed_parts(pre_act):
    activated = jnp.maximum(pre_act, 0.0)
    inverse = lax.rsqrt(jnp.mean(activated * activated, axis=1, keepdims=True) + epsilon)
    return (activated * inverse, activated, inverse)


def norm_backward(hidden_grad, activated, inverse, pre_act):
    inner_sum = jnp.mean(hidden_grad * activated, axis=1, keepdims=True)
    act_grad = inverse * hidden_grad - activated * (inverse * inverse * inverse) * inner_sum
    return jnp.where(pre_act > 0, act_grad, 0.0)


def body(
    stored_features,
    vertex_row_index,
    neighbors,
    counts,
    self_w1,
    neigh_w1,
    self_w2,
    neigh_w2,
    upstream,
):
    mp_index = lax.axis_index("mp")
    sampled_graphs = upstream.shape[0]
    own_rows = upstream.shape[1]
    row_grand_total = vertex_row_index.shape[0] // sampled_graphs
    column_total = stored_features.shape[1]
    slot_positions = neighbors.shape[2]
    gradient_scale = 1.0 / math.sqrt(row_grand_total * sampled_graphs * lax.axis_size("node"))
    first_row = mp_index * own_rows
    stored_blocks = stored_features.reshape(sampled_graphs, row_grand_total, column_total)
    vertex_blocks = vertex_row_index.reshape(sampled_graphs, row_grand_total)
    neighbor_blocks = jnp.transpose(
        neighbors.reshape(2, sampled_graphs, row_grand_total, slot_positions), (1, 0, 2, 3)
    )
    block_count = jnp.transpose(counts.reshape(2, sampled_graphs, row_grand_total), (1, 0, 2))

    def one_graph(carry, packed):
        store_rows, node_rows, neighbor_ids, row_counts, cotangent = packed
        features = jnp.take(store_rows, node_rows, axis=0)
        adj_zero = adjacency(neighbor_ids[0], row_counts[0], row_grand_total)
        agg_zero = jnp.dot(adj_zero, features, precision=precise)
        own_ids = lax.dynamic_slice_in_dim(neighbor_ids[1], first_row, own_rows, 0)
        own_counts = lax.dynamic_slice_in_dim(row_counts[1], first_row, own_rows, 0)
        adj_own = adjacency(own_ids, own_counts, row_grand_total)
        scaled = cotangent * gradient_scale
        back_neigh = jnp.dot(scaled, neigh_w2.T, precision=precise)
        back_self = jnp.dot(scaled, self_w2.T, precision=precise)
        contrib = lax.dot_general(adj_own, back_neigh, (((0,), (0,)), ((), ())), precision=precise)
        rows_self = features
        rows_neigh = agg_zero
        pre_own = lax.psum_scatter(
            jnp.dot(rows_self, self_w1, precision=precise)
            + jnp.dot(rows_neigh, neigh_w1, precision=precise),
            "mp",
            scatter_dimension=0,
            tiled=True,
        )
        hidden_own, act_own, inverse_own = normed_parts(pre_own)
        hidden_all = lax.all_gather(hidden_own, "mp", axis=0, tiled=True)
        agg_one = jnp.dot(adj_own, hidden_all, precision=precise)
        hidden_grad = lax.psum_scatter(contrib, "mp", scatter_dimension=0, tiled=True) + back_self
        pre_grad = norm_backward(hidden_grad, act_own, inverse_own, pre_own)
        grad_piece = lax.all_gather(pre_grad, "mp", axis=0, tiled=True)
        rows_self = features
        rows_neigh = agg_zero
        step_self1 = carry[0] + jnp.dot(rows_self.T, grad_piece, precision=precise)
        step_neigh1 = carry[1] + jnp.dot(rows_neigh.T, grad_piece, precision=precise)
        graph_out = jnp.dot(hidden_own, self_w2, precision=precise) + jnp.dot(
            agg_one, neigh_w2, precision=precise
        )
        step_self2 = carry[2] + jnp.dot(hidden_own.T, scaled, precision=precise)
        step_neigh2 = carry[3] + jnp.dot(agg_one.T, scaled, precision=precise)
        return ((step_self1, step_neigh1, step_self2, step_neigh2), graph_out)

    zero_first = jnp.zeros(self_w1.shape, jnp.float32)
    zero_second = jnp.zeros(self_w2.shape, jnp.float32)
    totals, layer_out = lax.scan(
        one_graph,
        (zero_first, zero_first, zero_second, zero_second),
        (stored_blocks, vertex_blocks, neighbor_blocks, block_count, upstream),
    )
    grad_self1, grad_neigh1, grad_self2, grad_neigh2 = totals
    grad_self1, grad_neigh1, grad_self2, grad_neigh2 = lax.psum(
        (grad_self1, grad_neigh1, grad_self2, grad_neigh2), "node"
    )
    grad_self2, grad_neigh2 = lax.psum((grad_self2, grad_neigh2), "mp")
    return (layer_out, grad_self1, grad_neigh1, grad_self2, grad_neigh2)


f32 = jnp.float32
bf16 = jnp.bfloat16


def halves(value):
    high = value.astype(bf16)
    return high, (value - high.astype(f32)).astype(bf16)


def thirds(value):
    high = value.astype(bf16)
    rest = value - high.astype(f32)
    middle = rest.astype(bf16)
    return high, middle, (rest - middle.astype(f32)).astype(bf16)


def mul(left, right, dims=((1,), (0,))):
    return lax.dot_general(left, right, (dims, ((), ())), preferred_element_type=f32)


def mul3(left, right, dims=((1,), (0,))):
    return (
        mul(left[0], right[0], dims) + mul(left[1], right[0], dims) + mul(left[0], right[1], dims)
    )


def mul6(left, right):
    small = mul(left[2], right[0]) + mul(left[0], right[2]) + mul(left[1], right[1])
    return mul(left[0], right[0]) + (mul(left[0], right[1]) + mul(left[1], right[0]) + small)


def fused_kernel(
    node_total,
    slots,
    scale,
    store_ref,
    nbr_ref,
    vertex_ref,
    counts_ref,
    s1_ref,
    n1_ref,
    s2_ref,
    n2_ref,
    up_ref,
    out_ref,
    g1_ref,
    g2_ref,
    upg,
    part,
    pin,
    far,
    pg,
    xh,
    xl,
    xt,
    wh,
    wl,
    wt,
    ids_t,
    ids,
    onehot,
    adj,
    act_buf,
    g1acc,
    g2acc,
    g2in,
    q2,
    q2r,
    outg,
    xin,
    xhalf,
    zin,
    send_sems,
    recv_sems,
):
    rows = upg.shape[0]
    own = up_ref.shape[1]
    cols = store_ref.shape[1]
    depth = node_total // 2
    node = lax.axis_index("node")
    member = lax.axis_index("mp")
    zc, xc = node // 2, node % 2
    yc, cc = member // 2, member % 2
    partner = yc * 2 + (1 - cc)
    across = (1 - yc) * 2 + cc
    diagonal = (1 - yc) * 2 + (1 - cc)
    peers = (partner, across, diagonal)
    x_peer = zc * 2 + (1 - xc)
    z_next = [((zc + d) % depth) for d in range(1, depth)]
    z_prev = [((zc + depth - d) % depth) for d in range(1, depth)]

    def target(node_id, member_id):
        return dict(device_id=(node_id, member_id), device_id_type=pl.DeviceIdType.MESH)

    counter = [0]

    def copy(source, dest, node_id, member_id):
        k = counter[0]
        counter[0] += 1
        return pltpu.make_async_remote_copy(
            src_ref=source,
            dst_ref=dest,
            send_sem=send_sems.at[k],
            recv_sem=recv_sems.at[k],
            **target(node_id, member_id),
        )

    barrier = pltpu.get_barrier_semaphore()
    for p in peers:
        pl.semaphore_signal(barrier, inc=1, **target(node, p))
    pl.semaphore_signal(barrier, inc=1, **target(x_peer, member))
    for z in z_next:
        pl.semaphore_signal(barrier, inc=1, **target(z * 2 + xc, member))
    pl.semaphore_wait(barrier, 4 + depth - 1)

    def block(index, size):
        return pl.ds(pl.multiple_of(index * size, size), size)

    ids_t[...] = jnp.zeros_like(ids_t)
    up_copies = [copy(up_ref.at[p], upg.at[block(member, own)], node, p) for p in peers]
    for one in up_copies:
        one.start()
    upg[block(member, own)] = up_ref[member]
    wh[:cols], wl[:cols], wt[:cols] = thirds(s1_ref[...])
    wh[cols:], wl[cols:], wt[cols:] = thirds(n1_ref[...])

    tile = 64
    middle = rows // 2
    lanes = (lax.broadcasted_iota(jnp.int32, (tile, rows), 1) - middle).astype(f32).astype(bf16)
    one_b, none_b = jnp.ones((), bf16), jnp.zeros((), bf16)

    def hits(picked, first):
        total = jnp.zeros((tile, rows), bf16)
        for k in range(first, first + slots):
            total = total + jnp.where(picked[:, k : k + 1] == lanes, one_b, none_b)
        return total

    def stage_ids(graph):
        span = block(graph, rows)
        slot = lax.broadcasted_iota(jnp.int32, (slots, rows), 0)
        for layer in range(2):
            used = slot < counts_ref[layer : layer + 1, span]
            ids_t[layer * slots : (layer + 1) * slots] = jnp.where(
                used, nbr_ref[layer, :, span], 4 * rows
            )
        ids_t[2 * slots : 2 * slots + 1] = vertex_ref[:, span]
        ids_t[2 * slots + 1 : 2 * slots + 3] = counts_ref[:, span]
        ids[...] = jnp.transpose(ids_t[...])

    def build(first, with_vertex):
        @pl.loop(0, rows // tile)
        def _(t):
            picked = (ids[block(t, tile)] - middle).astype(f32).astype(bf16)
            to = block(t, tile)
            adj[to] = hits(picked, first)
            if with_vertex:
                v = 2 * slots
                onehot[to] = jnp.where(picked[:, v : v + 1] == lanes, one_b, none_b)

    def reciprocal(layer):
        k = 2 * slots + 1 + layer
        return 1.0 / ids[:, k : k + 1].astype(f32)

    to_partner_a = copy(part.at[0], pin.at[0], node, partner)
    to_across = copy(part.at[1], far, node, across)
    to_partner_b = copy(part.at[2], pin.at[1], node, partner)

    @pl.loop(0, 4)
    def _(s):
        gy = yc + (1 - s // 2) * (1 - 2 * yc)
        gc = cc + (1 - s % 2) * (1 - 2 * cc)
        graph = gy * 2 + gc
        stage_ids(graph)
        build(0, True)
        sh, sl, st = thirds(store_ref[block(graph, rows)])
        fh = mul(onehot[...], sh).astype(bf16)
        fl = mul(onehot[...], sl).astype(bf16)
        ft = mul(onehot[...], st).astype(bf16)
        xh[s, :, :cols] = fh
        xl[s, :, :cols] = fl
        xt[:, :cols] = ft
        agg = (mul(adj[...], ft) + mul(adj[...], fl) + mul(adj[...], fh)) * reciprocal(0)
        ah, al, at = thirds(agg)
        xt[:, cols:] = at
        xh[s, :, cols:] = ah
        xl[s, :, cols:] = al
        part[s] = mul6((xh[s], xl[s], xt[...]), (wh[...], wl[...], wt[...]))

        @pl.when(s == 0)
        def _():
            to_partner_a.start()

        @pl.when(s == 1)
        def _():
            to_partner_a.wait_recv()
            part[1] = part[1] + pin[0]
            to_across.start()

        @pl.when(s == 2)
        def _():
            to_partner_b.start()

    build(slots, False)
    shrink = reciprocal(1)
    for one in up_copies:
        one.wait_recv()
    scaled = halves(upg[...] * scale)
    w2s = halves(s2_ref[...])
    w2n = halves(n2_ref[...])
    nt = ((1,), (1,))
    tn = ((0,), (0,))
    back = halves(mul3(scaled, w2n, nt) * shrink)
    hidden_grad = mul3(scaled, w2s, nt) + mul(adj[...], back[0], tn) + mul(adj[...], back[1], tn)
    act_buf[...] = hidden_grad
    to_partner_b.wait_recv()
    near = part[3] + pin[1]
    to_across.wait_recv()
    pre = near + far[...]
    hidden, activated, inverse = normed_parts(pre)
    pg[3] = norm_backward(act_buf[...], activated, inverse, pre)
    pg_partner = copy(pg.at[3], pg.at[2], node, partner)
    parts = [pl.ds(i * own, own) for i in range(4)]
    pg_across = [copy(pg.at[3, r], pg.at[1, r], node, across) for r in parts]
    pg_forward = [copy(pg.at[1, r], pg.at[0, r], node, partner) for r in parts]
    for one in pg_across:
        one.start()
    pg_partner.start()

    hid = halves(hidden)
    agg_one = halves((mul(adj[...], hid[0]) + mul(adj[...], hid[1])) * shrink)
    width = hidden.shape[1]
    scaled = halves(upg[...] * scale)
    g2acc[:width] = mul3(hid, scaled, tn)
    g2acc[width:] = mul3(agg_one, scaled, tn)
    quarter = g2acc.shape[0] // 4
    g2_copies = [
        copy(g2acc.at[block(p, quarter)], g2in.at[d], node, p) for d, p in enumerate(peers)
    ]
    for one in g2_copies:
        one.start()
    w2s = halves(s2_ref[...])
    w2n = halves(n2_ref[...])
    outg[...] = mul3(hid, w2s) + mul3(agg_one, w2n)
    out_copies = [copy(outg.at[block(p, own)], out_ref.at[member], node, p) for p in peers]
    for one in out_copies:
        one.start()
    out_ref[member] = outg[block(member, own)]

    g1acc[...] = jnp.zeros_like(g1acc)

    @pl.loop(0, 4)
    def _(t):
        s = 3 - t

        @pl.when(t == 1)
        def _():
            pg_partner.wait_recv()

        @pl.when(t == 2)
        def _():
            for one, onward in zip(pg_across, pg_forward):
                one.wait_recv()
                onward.start()

        @pl.when(t == 3)
        def _():
            for one in pg_forward:
                one.wait_recv()

        g1acc[...] += mul3((xh[s], xl[s]), halves(pg[s]), tn)

    sets = []
    chunk = q2.shape[0]
    pieces = g1acc.shape[0] // chunk
    for full, base, i, result in [(g1acc, e * chunk, e, g1_ref) for e in range(pieces)] + [
        (q2, 0, pieces, q2r)
    ]:
        size = chunk // 2
        piece = size // depth
        x_in, half, z_in = xin.at[i], xhalf.at[i], zin.at[i]
        away = pl.ds(pl.multiple_of(base + (1 - xc) * size, size), size)
        home = pl.ds(pl.multiple_of(base + xc * size, size), size)
        x_copy = copy(full.at[away], x_in, x_peer, member)
        z_copies = [
            copy(xhalf.at[i, block(z, piece)], zin.at[i, d], z * 2 + xc, member)
            for d, z in enumerate(z_next)
        ]
        mine = pl.ds(pl.multiple_of(base + xc * size + zc * piece, piece), piece)
        spread = [copy(result.at[mine], result.at[mine], z * 2 + xc, member) for z in z_next]
        echo = [copy(result.at[mine], result.at[mine], x_peer, member)]
        for z in z_prev:
            there = pl.ds(pl.multiple_of(base + xc * size + z * piece, piece), piece)
            echo.append(copy(result.at[there], result.at[there], x_peer, member))
        sets.append((full, home, i, piece, result, x_copy, z_copies, mine, spread, echo))

    def start_z(one):
        full, home, i, piece, result, x_copy, z_copies = one[:7]
        x_copy.wait()
        xhalf[i] = full[home] + xin[i]
        for each in z_copies:
            each.start()

    def start_spread(one):
        full, home, i, piece, result, x_copy, z_copies, mine, spread, echo = one
        total = xhalf[i, block(zc, piece)]
        for d, each in enumerate(z_copies):
            each.wait_recv()
            total = total + zin[i, d]
        result[mine] = total
        for each in spread:
            each.start()
        echo[0].start()

    def relay(one):
        for each, onward in zip(one[8], one[9][1:]):
            each.wait_recv()
            onward.start()

    def finish(one):
        for each in one[9]:
            each.wait()
        for each in one[6] + one[8]:
            each.wait_send()

    first, second = sets[:-1], sets[-1]
    for one in first:
        one[5].start()
    for one in first[:-1]:
        start_z(one)
    summed = g2acc[block(member, quarter)]
    for d, one in enumerate(g2_copies):
        one.wait_recv()
        summed = summed + g2in[d]
    q2[...] = summed
    second[5].start()
    start_z(first[-1])
    for one in first:
        start_spread(one)
    start_z(second)
    for one in first:
        relay(one)
    start_spread(second)
    relay(second)
    finish(second)
    here = block(member, quarter)
    last = [copy(q2r, g2_ref.at[here], node, p) for p in peers]
    for one in last:
        one.start()
    g2_ref[here] = q2r[...]
    for one in first:
        finish(one)
    for one in up_copies + [to_partner_a, to_across, to_partner_b, pg_partner] + pg_across + pg_forward:
        one.wait_send()
    for one in g2_copies:
        one.wait_send()
    for one in out_copies + last:
        one.wait()


def fused(mesh_node):
    def run(stored, vertex, neighbors, counts, self_w1, neigh_w1, self_w2, neigh_w2, upstream):
        graphs, own, width = upstream.shape
        rows = vertex.shape[0] // graphs
        slots = neighbors.shape[2]
        cols = stored.shape[1]
        total = vertex.shape[0]
        turned = jnp.transpose(neighbors, (0, 2, 1))
        scale = 1.0 / math.sqrt(total * mesh_node)
        depth = mesh_node // 2
        wide = 2 * cols
        quarter = 2 * width // 4
        groups = wide // quarter + 1
        copies = 24 + groups * (2 + 3 * (depth - 1))
        vm = pltpu.VMEM
        scratch = [
            vm((rows, width), f32),
            vm((4, rows, width), f32),
            vm((2, rows, width), f32),
            vm((rows, width), f32),
            vm((4, rows, width), f32),
            vm((4, rows, wide), bf16),
            vm((4, rows, wide), bf16),
            vm((rows, wide), bf16),
            vm((wide, width), bf16),
            vm((wide, width), bf16),
            vm((wide, width), bf16),
            vm((128, rows), jnp.int32),
            vm((rows, 128), jnp.int32),
            vm((rows, rows), bf16),
            vm((rows, rows), bf16),
            vm((rows, width), f32),
            vm((wide, width), f32),
            vm((2 * width, width), f32),
            vm((3, quarter, width), f32),
            vm((quarter, width), f32),
            vm((quarter, width), f32),
            vm((rows, width), f32),
            vm((groups, quarter // 2, width), f32),
            vm((groups, quarter // 2, width), f32),
            vm((groups, depth - 1, quarter // 2 // depth, width), f32),
            pltpu.SemaphoreType.DMA((copies,)),
            pltpu.SemaphoreType.DMA((copies,)),
        ]
        space = pl.BlockSpec(memory_space=pltpu.VMEM)
        out, g1, g2 = pl.pallas_call(
            functools.partial(fused_kernel, mesh_node, slots, scale),
            out_shape=(
                jax.ShapeDtypeStruct((graphs, own, width), f32),
                jax.ShapeDtypeStruct((wide, width), f32),
                jax.ShapeDtypeStruct((2 * width, width), f32),
            ),
            in_specs=[space] * 9,
            out_specs=(space,) * 3,
            scratch_shapes=scratch,
            compiler_params=pltpu.CompilerParams(
                collective_id=0, has_side_effects=True, vmem_limit_bytes=60 * 1024 * 1024
            ),
        )(stored, turned, vertex[None], counts, self_w1, neigh_w1, self_w2, neigh_w2, upstream)
        return out, g1[:cols], g1[cols:], g2[:width], g2[width:]

    return run


def fitted(mesh):
    node_total, members = mesh.shape["node"], mesh.shape["mp"]

    def run(*args):
        vertex, upstream, stored = args[1], args[8], args[0]
        graphs, own, width = upstream.shape
        depth = node_total // 2
        fits = (
            members == 4
            and graphs == members
            and node_total % 2 == 0
            and depth > 1
            and own * members * graphs == vertex.shape[0]
            and own % 64 == 0
            and own * members <= 512
            and 2 * args[2].shape[2] + 3 <= 128
            and args[2].shape[2] % 8 == 0
            and width % 128 == 0
            and stored.shape[1] % 128 == 0
            and (width // 4) % (8 * depth) == 0
            and (2 * stored.shape[1]) % (width // 2) == 0
        )
        return (fused(node_total) if fits else body)(*args)

    return run


def solution(mesh):
    placed = (
        P("node", "mp"),
        P("node"),
        P(None, "node", None),
        P(None, "node"),
        P("mp", None),
        P("mp", None),
        P(),
        P(),
        P("node", "mp", None),
    )
    return jax.shard_map(
        fitted(mesh),
        mesh=mesh,
        in_specs=placed,
        out_specs=(P("node", "mp", None), P("mp", None), P("mp", None), P(), P()),
        check_vma=False,
    )
```
